32 devices in a mesh: req: 16 (over z, y, x), tp: 2 (over core).
Axes of the slice: x: 2, y: 2, z: 4, core: 2. Of those that a mesh axis runs over, the one named last changes fastest.
Arguments:
- hidden: bfloat16 [384, 4096], P('req', 'tp'), may hold values from -100 to 100
- norm_gain: float32 [4096], replicated, may hold values from 0.5 to 1.5
- norm_bias: float32 [4096], replicated, may hold values from -3 to 3
- unembed: bfloat16 [3136, 4096], P(('req', 'tp')), as said below
- targets: int32 [384], P('req'), may hold values from 0 to 3135
- span_start: int32 [48], P('req'), may hold values from 0 to 24, as said below
- span_end: int32 [48], P('req'), may hold values from 0 to 24, as said below
Outputs:
- logprob: float32 [384], P('req')
- entropy: float32 [384], P('req')
The draws below stay inside these ranges and needn't reach their ends.
Inputs may be any that keep to these rules, and one draw needn't show every extreme that they name: A device's 3 spans are entries i * 3 to i * 3 + 2 of span_start and span_end; they are ordered and disjoint within its 24 rows, with start <= end (a span may be empty). Summed over all req devices, the rows inside spans number 12 times the number of req devices; a single device may hold from 1 to 24 of them, and on at least one device all 24 rows are inside spans. `span_end`: paired with span_start as stated there. `unembed`: entries lie within 20 / sqrt(4096) + 1600 / 4096 in magnitude.
All inputs are finite; a program needn't handle non-finite values.
Results may differ from the reference program's by a relative error of at most 0.0029.
Values may be sent and summed in bfloat16 or wider, within the bound.
No kernel may reach another device: no remote copies, remote signals or barrier semaphores. Data moves between devices by JAX's collectives and lax.ppermute only.
A program may use at most 64 MiB of HBM per device.

```python
import math
import jax
import jax.numpy as jnp
import numpy as np
from jax import lax

D = 4096
SLOTS = 24
REQ_DEV = 3
LIVE_DEV = 12
ROWS = 384
VOCAB = 3136
N_REQ = 16


def drawn_directions(key):
    return jnp.clip(jax.random.normal(jax.random.fold_in(key, 7), (4, D), jnp.float32), -4.0, 4.0)


def draw_hidden(key, part):
    key_base, key_col, key_row = jax.random.split(jax.random.fold_in(key, 3), 3)
    col_ramp = jnp.sqrt(1.0 + 2.0 * jnp.arange(D, dtype=jnp.float32) / (D - 1))
    col_scale = 10.0 ** (jax.random.uniform(key_col, (1, D), jnp.float32) - 0.5) * col_ramp
    row_scale = 10.0 ** (jax.random.uniform(key_row, (ROWS, 1), jnp.float32) - 0.5)
    values = jnp.clip(jax.random.normal(key_base, (ROWS, D), jnp.float32), -4.0, 4.0) * col_scale * row_scale
    row_index = jnp.arange(ROWS)
    direction_id = row_index // 16 % 4
    aligned = drawn_directions(key)[direction_id]
    values = jnp.where((row_index % 16 == 3)[:, None], aligned, values)
    return values.astype(jnp.bfloat16)


def draw_unembed(key, part):
    key_main = jax.random.fold_in(jax.random.fold_in(key, 5), 0)
    width_root = math.sqrt(D)
    values = jnp.clip(jax.random.normal(key_main, (VOCAB, D), jnp.float32), -4.0, 4.0) * (3.0 / width_root)
    directions = drawn_directions(key)
    strength = jnp.array([150.0, 210.0, 300.0, 400.0], jnp.float32)
    strong_rows = directions * (strength[:, None] / D)
    near_rows = strong_rows * (1.0 - 2.0 / strength[:, None])
    strong_index = jnp.arange(4) * VOCAB // 4 + 2
    values = values.at[strong_index].set(strong_rows).at[strong_index + 1].set(near_rows)
    return values.astype(jnp.bfloat16)


def span_layout(key):
    key_pos, key_dev, key_cut, key_gap = jax.random.split(jax.random.fold_in(key, 11), 4)
    devices = ROWS // SLOTS
    others = devices - 1
    cell_count = others * (SLOTS - 1)
    extra_balls = LIVE_DEV * devices - SLOTS - others
    cell_order = jax.random.permutation(key_pos, cell_count)[:extra_balls]
    owner_rank = cell_order // (SLOTS - 1)
    rest_counts = 1 + jnp.sum((owner_rank[:, None] == jnp.arange(others)[None, :]).astype(jnp.int32), axis=0)
    counts = jnp.concatenate([jnp.full((1,), SLOTS, jnp.int32), rest_counts.astype(jnp.int32)])
    counts = jax.random.permutation(key_dev, counts)
    len_cuts = jnp.sort(jax.random.randint(key_cut, (devices, REQ_DEV - 1), 0, counts[:, None] + 1), axis=1)
    len_edges = jnp.concatenate([jnp.zeros((devices, 1), jnp.int32), len_cuts.astype(jnp.int32), counts[:, None]], axis=1)
    lengths = len_edges[:, 1:] - len_edges[:, :-1]
    gap_cuts = jnp.sort(jax.random.randint(key_gap, (devices, REQ_DEV), 0, SLOTS - counts[:, None] + 1), axis=1)
    starts = gap_cuts.astype(jnp.int32) + len_edges[:, :-1]
    return (starts.reshape(-1).astype(jnp.int32), (starts + lengths).reshape(-1).astype(jnp.int32))


def draw_span_start(key, part):
    return span_layout(key)[0]


def draw_span_end(key, part):
    return span_layout(key)[1]


def plant(result, stream_key, low, high):
    spot = [jax.random.randint(jax.random.fold_in(stream_key, axis), (), 0, length) for axis, length in enumerate(result.shape)]
    main_axis = result.shape.index(max(result.shape))
    neighbour = spot[:main_axis] + [(spot[main_axis] + 1) % result.shape[main_axis]] + spot[main_axis + 1:]
    return result.at[tuple(spot)].set(low).at[tuple(neighbour)].set(high)


def rank_bounds(count, slope):
    weights = [(1 << 20) // math.isqrt(standing ** slope) + 1 for standing in range(1, count + 1)]
    spread = 1 + sum(weights) // (1 << 30)
    return np.cumsum(np.array([max(1, weight // spread) for weight in weights]))


def ranked_ids(rng, extent, amount, skew):
    grid = rank_bounds(amount, skew)
    ticket = jax.random.randint(jax.random.fold_in(rng, 1), extent, 0, int(grid[amount - 1]))
    grade = jnp.searchsorted(jnp.asarray(grid, jnp.int32), ticket, side="right")
    return jax.random.permutation(jax.random.fold_in(rng, 2), amount)[grade].astype(jnp.int32)


def normal_values(stream_key, shape, width, most, kind=jnp.bfloat16):
    return jnp.clip(width * jax.random.normal(stream_key, shape, jnp.float32), -most, most).astype(kind)


def setup_inputs(seed: int = 0) -> dict:
    splits = jax.random.split(jax.random.key(seed), 8)
    return {
        "hidden": draw_hidden(jax.random.fold_in(splits[7], 71), 0),
        "norm_gain": jnp.clip(1.0 + 0.1 * jax.random.normal(splits[1], (D,), jnp.float32), 0.5, 1.5),
        "norm_bias": normal_values(splits[2], (D,), 0.5, 3.0, jnp.float32),
        "unembed": draw_unembed(jax.random.fold_in(splits[7], 71), 0),
        "targets": plant(ranked_ids(splits[4], (ROWS,), VOCAB, 2), jax.random.fold_in(splits[4], 3), 0, VOCAB - 1).astype(jnp.int32),
        "span_start": draw_span_start(jax.random.fold_in(splits[7], 71), 0),
        "span_end": draw_span_end(jax.random.fold_in(splits[7], 71), 0),
    }


EPSILON = 1e-05

def live_mask(span_start, span_end, slot_count):
    position = jnp.arange(slot_count, dtype=jnp.int32)
    inside = (span_start[..., None] <= position) & (position < span_end[..., None])
    return jnp.any(inside, axis=-2)

def normalize(hidden, norm_gain, norm_bias):
    values = hidden.astype(jnp.float32)
    feature_count = values.shape[1]
    row_mean = lax.optimization_barrier(jnp.sum(values, axis=1, keepdims=True)) / feature_count
    row_square = lax.optimization_barrier(jnp.sum(values * values, axis=1, keepdims=True)) / feature_count
    scaled = (values - row_mean) * lax.rsqrt(row_square - row_mean * row_mean + EPSILON)
    return (scaled * norm_gain + norm_bias).astype(jnp.bfloat16)

def reference(hidden, norm_gain, norm_bias, unembed, targets, span_start, span_end):
    normed = normalize(hidden, norm_gain, norm_bias)
    block_size = VOCAB // N_REQ

    def block_step(running, block_index):
        row_top, row_total, row_spread, target_hit = running
        first_row = (block_index * block_size).astype(jnp.int32)
        block_rows = lax.dynamic_slice_in_dim(unembed, first_row, block_size, 0)
        scores = lax.dot_general(block_rows, normed, (((1,), (1,)), ((), ())), preferred_element_type=jnp.float32)
        new_top = jnp.maximum(row_top, lax.optimization_barrier(jnp.max(scores, axis=0)))
        decay_old = jnp.exp(row_top - new_top)
        weights = jnp.exp(scores - new_top)
        next_total = row_total * decay_old + lax.optimization_barrier(jnp.sum(weights, axis=0))
        next_spread = decay_old * (row_spread + row_total * (row_top - new_top)) + lax.optimization_barrier(jnp.sum(weights * (scores - new_top), axis=0))
        vocab_ids = first_row + jnp.arange(block_size, dtype=jnp.int32)
        next_hit = target_hit + lax.optimization_barrier(jnp.sum(jnp.where(vocab_ids[:, None] == targets[None, :], scores, 0.0), axis=0))
        return ((new_top, next_total, next_spread, next_hit), None)
    initial = (jnp.full((ROWS,), -1e+30, jnp.float32), jnp.zeros((ROWS,), jnp.float32), jnp.zeros((ROWS,), jnp.float32), jnp.zeros((ROWS,), jnp.float32))
    final_state, unused = lax.scan(block_step, initial, jnp.arange(N_REQ, dtype=jnp.int32))
    row_top, row_total, row_spread, target_hit = final_state
    log_total = jnp.log(row_total)
    live = live_mask(span_start.reshape(N_REQ, REQ_DEV), span_end.reshape(N_REQ, REQ_DEV), SLOTS).reshape(ROWS)
    logprob = jnp.where(live, target_hit - row_top - log_total, 0.0)
    entropy = jnp.where(live, log_total - row_spread / row_total, 0.0)
    return (logprob, entropy)
```

```python
import jax
import jax.numpy as jnp
from jax import lax
from jax.sharding import PartitionSpec as P

EPSILON = 1e-05


def live_mask(span_start, span_end, slot_count):
    position = jnp.arange(slot_count, dtype=jnp.int32)
    inside = (span_start[..., None] <= position) & (position < span_end[..., None])
    return jnp.any(inside, axis=-2)


def normalize(hidden, norm_gain, norm_bias):
    values = hidden.astype(jnp.float32)
    feature_count = values.shape[1]
    row_mean = jnp.sum(values, axis=1, keepdims=True) / feature_count
    row_square = jnp.sum(values * values, axis=1, keepdims=True) / feature_count
    scaled = (values - row_mean) * lax.rsqrt(row_square - row_mean * row_mean + EPSILON)
    return (scaled * norm_gain + norm_bias).astype(jnp.bfloat16)


def gathered(hidden, norm_gain, norm_bias, unembed, targets, span_start, span_end):
    slot_count = hidden.shape[0]
    tp_count = lax.axis_size("tp")
    req_rank = lax.axis_index("req")
    tp_rank = lax.axis_index("tp")
    vocab_part = unembed.shape[0]
    vocab_first = (req_rank * tp_count + tp_rank) * vocab_part
    live_mine = live_mask(span_start.reshape(1, -1), span_end.reshape(1, -1), slot_count).reshape(
        -1
    )
    row_ids = lax.all_gather(targets, "req", axis=0, tiled=True)
    full_rows = lax.all_gather(hidden, "tp", axis=1, tiled=True)
    normed = normalize(full_rows, norm_gain, norm_bias)
    scores = lax.dot_general(
        unembed,
        lax.all_gather(normed, "req", axis=0, tiled=True),
        (((1,), (1,)), ((), ())),
        preferred_element_type=jnp.float32,
    )
    vocab_ids = vocab_first + jnp.arange(vocab_part, dtype=jnp.int32)
    target_hit = jnp.sum(jnp.where(vocab_ids[:, None] == row_ids[None, :], scores, 0.0), axis=0)
    row_top = lax.pmax(jnp.max(scores, axis=0), ("req", "tp"))
    weights = jnp.exp(scores - row_top)
    row_total, row_spread, target_hit = lax.psum(
        (jnp.sum(weights, axis=0), jnp.sum(weights * (scores - row_top), axis=0), target_hit),
        ("req", "tp"),
    )
    log_total = jnp.log(row_total)
    logprob_all = target_hit - row_top - log_total
    entropy_all = log_total - row_spread / row_total
    logprob_mine = lax.dynamic_slice_in_dim(logprob_all, req_rank * slot_count, slot_count)
    entropy_mine = lax.dynamic_slice_in_dim(entropy_all, req_rank * slot_count, slot_count)
    return (jnp.where(live_mine, logprob_mine, 0.0), jnp.where(live_mine, entropy_mine, 0.0))


X_BIT, Y_BIT, Z_NEAR, Z_FAR = 1, 2, 4, 8


def exchange(value, bits):
    pairs = [
        (chip * 2 + core, (chip ^ bits[core]) * 2 + core) for chip in range(16) for core in range(2)
    ]
    return lax.ppermute(value, ("req", "tp"), pairs)


def core_swap(value):
    return lax.ppermute(value, "tp", [(0, 1), (1, 0)])


ROW_STAGES = ((Z_FAR, Z_FAR), (X_BIT, Y_BIT), (Y_BIT, X_BIT))


def block_partials(rows, row_ids, blocks, firsts):
    scores = [
        lax.dot_general(
            block, rows, (((1,), (1,)), ((), ())), preferred_element_type=jnp.float32
        )
        for block in blocks
    ]
    top = jnp.max(scores[0], axis=0)
    for part in scores[1:]:
        top = jnp.maximum(top, jnp.max(part, axis=0))
    total = jnp.zeros_like(top)
    spread = jnp.zeros_like(top)
    hit = jnp.zeros_like(top)
    for part, first in zip(scores, firsts):
        shifted = part - top
        weights = jnp.exp(shifted)
        total += jnp.sum(weights, axis=0)
        spread += jnp.sum(weights * shifted, axis=0)
        ids = first + jnp.arange(part.shape[0], dtype=jnp.int32)
        hit += jnp.sum(jnp.where(ids[:, None] == row_ids[None, :], part, 0.0), axis=0)
    return jnp.stack([top, total, spread, hit])


def merge(one, two):
    top = jnp.maximum(one[0], two[0])
    down_one, down_two = one[0] - top, two[0] - top
    scale_one, scale_two = jnp.exp(down_one), jnp.exp(down_two)
    total = scale_one * one[1] + scale_two * two[1]
    spread = scale_one * (one[2] + one[1] * down_one) + scale_two * (two[2] + two[1] * down_two)
    return jnp.stack([top, total, spread, one[3] + two[3]])


def paired(hidden, norm_gain, norm_bias, unembed, targets, span_start, span_end):
    slot_count, feature_part = hidden.shape
    half = slot_count // 2
    width = 2 * feature_part
    req_rank = lax.axis_index("req")
    tp_rank = lax.axis_index("tp")
    first_core = tp_rank == 0
    vocab_part = unembed.shape[0]

    other = core_swap(hidden)
    near = exchange(unembed, (Z_NEAR, Z_NEAR))
    blocks = [unembed, core_swap(unembed), near, core_swap(near)]
    owners = [
        (chip * 2 + core)
        for chip in (req_rank, req_rank ^ Z_NEAR)
        for core in (tp_rank, 1 - tp_rank)
    ]
    firsts = [owner * vocab_part for owner in owners]

    def mine(value):
        return jnp.where(first_core, value[:half], value[half:])

    full_rows = jnp.where(
        first_core,
        jnp.concatenate([mine(hidden), mine(other)], axis=1),
        jnp.concatenate([mine(other), mine(hidden)], axis=1),
    )
    normed = normalize(full_rows, norm_gain, norm_bias)
    ids = mine(targets)
    id_columns = jnp.stack([ids // 256, ids % 256], axis=1).astype(jnp.bfloat16)
    rows = jnp.concatenate([normed, jnp.pad(id_columns, ((0, 0), (0, 126)))], axis=1)

    def partials(part):
        digits = part[:, width : width + 2].astype(jnp.int32)
        return block_partials(part[:, :width], digits[:, 0] * 256 + digits[:, 1], blocks, firsts)

    rows = jnp.concatenate([rows, exchange(rows, ROW_STAGES[0])], axis=0)
    rows = jnp.concatenate([rows, exchange(rows, ROW_STAGES[1])], axis=0)
    rows_far = exchange(rows, ROW_STAGES[2])
    stats = merge(partials(rows), exchange(partials(rows_far), ROW_STAGES[2]))
    for bits in ROW_STAGES[1::-1]:
        keep = stats.shape[1] // 2
        stats = merge(stats[:, :keep], exchange(stats[:, keep:], bits))
    log_total = jnp.log(stats[1])
    result = jnp.stack([stats[3] - stats[0] - log_total, log_total - stats[2] / stats[1]])
    partner = core_swap(result)
    both = jnp.where(
        first_core,
        jnp.concatenate([result, partner], axis=1),
        jnp.concatenate([partner, result], axis=1),
    )
    live = live_mask(span_start, span_end, slot_count)
    both = jnp.where(live, both, 0.0)
    return both[0], both[1]


def solution(mesh):
    chips_of_two = mesh.shape["req"] == 16 and mesh.shape["tp"] == 2
    return jax.shard_map(
        paired if chips_of_two else gathered,
        mesh=mesh,
        in_specs=(P("req", "tp"), P(), P(), P(("req", "tp"), None), P("req"), P("req"), P("req")),
        out_specs=(P("req"), P("req")),
        check_vma=False,
    )
```

```python
import functools

import jax
import jax.numpy as jnp
from jax import lax
from jax.experimental import pallas as pl
from jax.experimental.pallas import tpu as pltpu
from jax.sharding import PartitionSpec as P

EPSILON = 1e-05


def live_mask(span_start, span_end, slot_count):
    position = jnp.arange(slot_count, dtype=jnp.int32)
    inside = (span_start[..., None] <= position) & (position < span_end[..., None])
    return jnp.any(inside, axis=-2)


def normalize(hidden, norm_gain, norm_bias):
    values = hidden.astype(jnp.float32)
    feature_count = values.shape[1]
    row_mean = jnp.sum(values, axis=1, keepdims=True) / feature_count
    row_square = jnp.sum(values * values, axis=1, keepdims=True) / feature_count
    scaled = (values - row_mean) * lax.rsqrt(row_square - row_mean * row_mean + EPSILON)
    return (scaled * norm_gain + norm_bias).astype(jnp.bfloat16)


def gathered(hidden, norm_gain, norm_bias, unembed, targets, span_start, span_end):
    slot_count = hidden.shape[0]
    tp_count = lax.axis_size("tp")
    req_rank = lax.axis_index("req")
    tp_rank = lax.axis_index("tp")
    vocab_part = unembed.shape[0]
    vocab_first = (req_rank * tp_count + tp_rank) * vocab_part
    live_mine = live_mask(span_start.reshape(1, -1), span_end.reshape(1, -1), slot_count).reshape(
        -1
    )
    row_ids = lax.all_gather(targets, "req", axis=0, tiled=True)
    full_rows = lax.all_gather(hidden, "tp", axis=1, tiled=True)
    normed = normalize(full_rows, norm_gain, norm_bias)
    scores = lax.dot_general(
        unembed,
        lax.all_gather(normed, "req", axis=0, tiled=True),
        (((1,), (1,)), ((), ())),
        preferred_element_type=jnp.float32,
    )
    vocab_ids = vocab_first + jnp.arange(vocab_part, dtype=jnp.int32)
    target_hit = jnp.sum(jnp.where(vocab_ids[:, None] == row_ids[None, :], scores, 0.0), axis=0)
    row_top = lax.pmax(jnp.max(scores, axis=0), ("req", "tp"))
    weights = jnp.exp(scores - row_top)
    row_total, row_spread, target_hit = lax.psum(
        (jnp.sum(weights, axis=0), jnp.sum(weights * (scores - row_top), axis=0), target_hit),
        ("req", "tp"),
    )
    log_total = jnp.log(row_total)
    logprob_all = target_hit - row_top - log_total
    entropy_all = log_total - row_spread / row_total
    logprob_mine = lax.dynamic_slice_in_dim(logprob_all, req_rank * slot_count, slot_count)
    entropy_mine = lax.dynamic_slice_in_dim(entropy_all, req_rank * slot_count, slot_count)
    return (jnp.where(live_mine, logprob_mine, 0.0), jnp.where(live_mine, entropy_mine, 0.0))


X_BIT, Y_BIT, Z_NEAR, Z_FAR = 1, 2, 4, 8
FAR, FIRST, SECOND = (Z_FAR, Z_FAR), (X_BIT, Y_BIT), (Y_BIT, X_BIT)
LANES = 128
KERNEL_VMEM = 16 << 20
CHUNKS = (24, 40)


def exchange(value, bits):
    pairs = [
        (chip * 2 + core, (chip ^ bits[core]) * 2 + core) for chip in range(16) for core in range(2)
    ]
    return lax.ppermute(value, ("req", "tp"), pairs)


def core_swap(value):
    return lax.ppermute(value, "tp", [(0, 1), (1, 0)])


def in_vmem(value):
    return pltpu.with_memory_space_constraint(value, pltpu.VMEM)


def my_half(ref, half):
    value = ref[...].astype(jnp.float32)
    return jnp.where(lax.axis_index("tp") == 0, value[:half], value[half:])


def stage_kernel(cuts, half, hidden_in, gain_in, bias_in, unembed_in, ids_in, *refs):
    hidden_ref, gain_ref, bias_ref, digit_ref, *chunks = refs[:-2]
    ids_ref, sems = refs[-2:]
    pairs = [(ids_in, ids_ref), (hidden_in, hidden_ref), (gain_in, gain_ref), (bias_in, bias_ref)]
    pairs += [
        (unembed_in.at[pl.ds(start, chunk.shape[0]), :], chunk)
        for chunk, start in zip(chunks, cuts)
    ]
    copies = [pltpu.make_async_copy(*pair, sems.at[k]) for k, pair in enumerate(pairs)]
    for copy in copies:
        copy.start()
    copies[0].wait()
    core = lax.axis_index("tp")
    row = lax.broadcasted_iota(jnp.int32, (half, LANES), 0)
    lane = lax.broadcasted_iota(jnp.int32, (half, LANES), 1)
    digits = jnp.zeros((half, LANES), jnp.int32)
    for index in range(half):
        row_id = ids_ref[core * half + index]
        digit = jnp.where(lane == 0, row_id >> 8, jnp.where(lane == 1, row_id & 255, 0))
        digits = jnp.where(row == index, digit, digits)
    digit_ref[...] = digits.astype(jnp.float32).astype(jnp.bfloat16)
    for copy in copies[1:]:
        copy.wait()


def in_hbm(value):
    return pltpu.with_memory_space_constraint(value, pltpu.HBM)


def stage(hidden, norm_gain, norm_bias, unembed, targets, cuts):
    half = hidden.shape[0] // 2
    width = norm_gain.shape[0]
    vmem = pl.BlockSpec(memory_space=pltpu.VMEM)
    chunks = [
        pltpu.VMEM((stop - start, width), jnp.bfloat16) for start, stop in zip(cuts, cuts[1:])
    ]
    return pl.pallas_call(
        functools.partial(stage_kernel, cuts, half),
        out_shape=[
            pltpu.VMEM(hidden.shape, hidden.dtype),
            pltpu.VMEM((1, width), jnp.float32),
            pltpu.VMEM((1, width), jnp.float32),
            pltpu.VMEM((half, LANES), jnp.bfloat16),
            *chunks,
        ],
        in_specs=[pl.BlockSpec(memory_space=pltpu.HBM)] * 5,
        out_specs=[vmem] * (4 + len(chunks)),
        scratch_shapes=[
            pltpu.SMEM(targets.shape, jnp.int32),
            pltpu.SemaphoreType.DMA((4 + len(chunks),)),
        ],
        compiler_params=pltpu.CompilerParams(vmem_limit_bytes=KERNEL_VMEM),
        name="stage",
    )(
        *map(
            in_hbm, (hidden, norm_gain.reshape(1, -1), norm_bias.reshape(1, -1), unembed, targets)
        )
    )


def normalize_kernel(own_ref, other_ref, gain_ref, bias_ref, digit_ref, rows_ref):
    half, part = rows_ref.shape[0], own_ref.shape[1]
    first_core = lax.axis_index("tp") == 0
    own, other = my_half(own_ref, half), my_half(other_ref, half)
    low, high = jnp.where(first_core, own, other), jnp.where(first_core, other, own)
    sides = ((low, 0), (high, part))
    row_mean = sum(jnp.sum(side, axis=1, keepdims=True) for side, _ in sides) / (2 * part)
    row_square = sum(jnp.sum(side * side, axis=1, keepdims=True) for side, _ in sides) / (2 * part)
    scale = lax.rsqrt(row_square - row_mean * row_mean + EPSILON)
    for side, start in sides:
        columns = pl.ds(start, part)
        scaled = (side - row_mean) * scale
        rows_ref[:, columns] = (scaled * gain_ref[:, columns] + bias_ref[:, columns]).astype(
            jnp.bfloat16
        )
    rows_ref[:, pl.ds(2 * part, LANES)] = digit_ref[...]


def normalize_rows(own, other, gain, bias, digits):
    half, part = own.shape[0] // 2, own.shape[1]
    vmem = pl.BlockSpec(memory_space=pltpu.VMEM)
    return pl.pallas_call(
        normalize_kernel,
        out_shape=pltpu.VMEM((half, 2 * part + LANES), jnp.bfloat16),
        in_specs=[vmem] * 5,
        out_specs=vmem,
        compiler_params=pltpu.CompilerParams(vmem_limit_bytes=KERNEL_VMEM),
        name="normalize_rows",
    )(*map(in_vmem, (own, other, gain, bias, digits)))


def merge(one, two):
    top = jnp.maximum(one[0], two[0])
    down_one, down_two = one[0] - top, two[0] - top
    scale_one, scale_two = jnp.exp(down_one), jnp.exp(down_two)
    total = scale_one * one[1] + scale_two * two[1]
    spread = scale_one * (one[2] + one[1] * down_one) + scale_two * (two[2] + two[1] * down_two)
    return top, total, spread, one[3] + two[3]


def partials_kernel(places, vocab_part, pieces, *refs):
    count = len(places)
    piece_refs, blocks = refs[:pieces], refs[pieces : pieces + count]
    earlier, outs, rows_ref = refs[pieces + count : -3], refs[-3:-1], refs[-1]
    width = blocks[0].shape[1]
    row_count = rows_ref.shape[0]
    piece_rows = row_count // pieces
    for index, piece in enumerate(piece_refs):
        rows_ref[pl.ds(index * piece_rows, piece_rows), :] = piece[...]
    chip, core = lax.axis_index("req"), lax.axis_index("tp")

    lane = lax.broadcasted_iota(jnp.int32, (16, LANES), 1)
    pick = jnp.where(lane == 0, 256.0, jnp.where(lane == 1, 1.0, 0.0)).astype(jnp.bfloat16)
    contract = (((1,), (1,)), ((), ()))
    row_ids = lax.dot_general(
        pick, rows_ref[:, pl.ds(width, LANES)], contract, preferred_element_type=jnp.float32
    )[:1].astype(jnp.int32)
    rows = rows_ref[:, pl.ds(0, width)]
    scores = [
        lax.dot_general(block[...], rows, contract, preferred_element_type=jnp.float32)
        for block in blocks
    ]
    top = scores[0].max(axis=0, keepdims=True)
    for part in scores[1:]:
        top = jnp.maximum(top, part.max(axis=0, keepdims=True))
    total = jnp.zeros((1, row_count), jnp.float32)
    spread, hit = total, total
    for part, (chip_bit, core_bit, start) in zip(scores, places):
        shifted = part - top
        weights = jnp.exp(shifted)
        total += weights.sum(axis=0, keepdims=True)
        spread += (weights * shifted).sum(axis=0, keepdims=True)
        first = ((chip ^ chip_bit) * 2 + (core ^ core_bit)) * vocab_part + start
        ids = first + lax.broadcasted_iota(jnp.int32, (part.shape[0], 1), 0)
        hit += jnp.where(ids == row_ids, part, 0.0).sum(axis=0, keepdims=True)
    stats = (top, total, spread, hit)
    half = row_count // 2
    if earlier:
        before = [
            jnp.concatenate([ref[pl.ds(k, 1), :] for ref in earlier], axis=1) for k in range(4)
        ]
        stats = merge(before, stats)
    for k in range(4):
        outs[0][pl.ds(k, 1), :] = stats[k][:, :half]
        outs[1][pl.ds(k, 1), :] = stats[k][:, half:]


def partials(rows, blocks, places, vocab_part, earlier=()):
    row_count = len(rows) * rows[0].shape[0]
    half = row_count // 2
    vmem = pl.BlockSpec(memory_space=pltpu.VMEM)
    return pl.pallas_call(
        functools.partial(partials_kernel, places, vocab_part, len(rows)),
        out_shape=[pltpu.VMEM((4, half), jnp.float32)] * 2,
        in_specs=[vmem] * (len(rows) + len(blocks) + len(earlier)),
        out_specs=[vmem] * 2,
        scratch_shapes=[pltpu.VMEM((row_count, rows[0].shape[1]), jnp.bfloat16)],
        compiler_params=pltpu.CompilerParams(vmem_limit_bytes=KERNEL_VMEM),
        name="partials",
    )(*map(in_vmem, (*rows, *blocks, *earlier)))


def merge_kernel(group, mine_ref, theirs_ref, keep_ref, give_ref):
    mine, theirs = ([ref[pl.ds(k, 1), :] for k in range(4)] for ref in (mine_ref, theirs_ref))
    for k, value in enumerate(merge(mine, theirs)):
        pieces = [value[:, at : at + group] for at in range(0, value.shape[1], group)]
        keep_ref[pl.ds(k, 1), :] = jnp.concatenate(pieces[0::2], axis=1)
        give_ref[pl.ds(k, 1), :] = jnp.concatenate(pieces[1::2], axis=1)


def finish_kernel(mine_ref, theirs_ref, out_ref):
    mine, theirs = ([ref[pl.ds(k, 1), :] for k in range(4)] for ref in (mine_ref, theirs_ref))
    row_top, row_total, row_spread, target_hit = merge(mine, theirs)
    log_total = jnp.log(row_total)
    out_ref[pl.ds(0, 1), :] = target_hit - row_top - log_total
    out_ref[pl.ds(1, 1), :] = log_total - row_spread / row_total


def merge_and_split(mine, theirs, group):
    vmem = pl.BlockSpec(memory_space=pltpu.VMEM)
    return pl.pallas_call(
        functools.partial(merge_kernel, group),
        out_shape=[pltpu.VMEM((4, mine.shape[1] // 2), jnp.float32)] * 2,
        in_specs=[vmem] * 2,
        out_specs=[vmem] * 2,
        compiler_params=pltpu.CompilerParams(vmem_limit_bytes=KERNEL_VMEM),
        name="merge_and_split",
    )(in_vmem(mine), in_vmem(theirs))


def finish(mine, theirs):
    vmem = pl.BlockSpec(memory_space=pltpu.VMEM)
    return pl.pallas_call(
        finish_kernel,
        out_shape=pltpu.VMEM((2, mine.shape[1]), jnp.float32),
        in_specs=[vmem] * 2,
        out_specs=vmem,
        compiler_params=pltpu.CompilerParams(vmem_limit_bytes=KERNEL_VMEM),
        name="finish",
    )(in_vmem(mine), in_vmem(theirs))


def paired(hidden, norm_gain, norm_bias, unembed, targets, span_start, span_end):
    slot_count = hidden.shape[0]
    half = slot_count // 2
    vocab_part = unembed.shape[0]
    first_core = lax.axis_index("tp") == 0

    cuts = [0, *[sum(CHUNKS[: k + 1]) for k in range(len(CHUNKS))], vocab_part]
    other = core_swap(hidden)
    own_part, gain, bias, digits, *chunks = stage(
        hidden, norm_gain, norm_bias, unembed, targets, cuts
    )
    own = normalize_rows(own_part, other, gain, bias, digits)
    near = [exchange(chunk, (Z_NEAR, Z_NEAR)) for chunk in chunks]
    far = exchange(own, FAR)
    own_side = exchange(own, FIRST)
    far, own_side, near[0] = lax.optimization_barrier((far, own_side, near[0]))
    near_rows = jnp.concatenate([own, own_side], axis=0)
    near_across = exchange(near_rows, SECOND)
    far_side = exchange(far, FIRST)
    far_side, near_across, near[1] = lax.optimization_barrier((far_side, near_across, near[1]))
    far_rows = jnp.concatenate([far, far_side], axis=0)
    far_across = exchange(far_rows, SECOND)

    blocks, places = [unembed, core_swap(unembed)], [(0, 0, 0), (0, 1, 0)]
    for block, start in zip(near, cuts):
        if start != cuts[-2]:
            blocks += [block, core_swap(block)]
            places += [(Z_NEAR, 0, start), (Z_NEAR, 1, start)]
    rows = [near_rows, far_rows, near_across, far_across]
    early = partials(rows, blocks, places, vocab_part)
    last, early = lax.optimization_barrier((near[-1], early))
    blocks = [last, core_swap(last)]
    places = [(Z_NEAR, core_bit, cuts[-2]) for core_bit in (0, 1)]
    keep, give = partials(rows, blocks, places, vocab_part, early)
    keep, give = merge_and_split(keep, exchange(give, SECOND), half)
    keep, give = merge_and_split(keep, exchange(give, FIRST), half)
    result = finish(keep, exchange(give, FAR))
    partner = core_swap(result)
    both = jnp.where(
        first_core,
        jnp.concatenate([result, partner], axis=1),
        jnp.concatenate([partner, result], axis=1),
    )
    live = live_mask(span_start, span_end, slot_count)
    both = jnp.where(live, both, 0.0)
    return both[0], both[1]


def solution(mesh):
    chips_of_two = mesh.shape["req"] == 16 and mesh.shape["tp"] == 2
    return jax.shard_map(
        paired if chips_of_two else gathered,
        mesh=mesh,
        in_specs=(P("req", "tp"), P(), P(), P(("req", "tp"), None), P("req"), P("req"), P("req")),
        out_specs=(P("req"), P("req")),
        check_vma=False,
    )
```

```python
import functools

import jax
import jax.numpy as jnp
from jax import lax
from jax.experimental import pallas as pl
from jax.experimental.pallas import tpu as pltpu
from jax.sharding import PartitionSpec as P

EPSILON = 1e-05


def live_mask(span_start, span_end, slot_count):
    position = jnp.arange(slot_count, dtype=jnp.int32)
    inside = (span_start[..., None] <= position) & (position < span_end[..., None])
    return jnp.any(inside, axis=-2)


def normalize(hidden, norm_gain, norm_bias):
    values = hidden.astype(jnp.float32)
    feature_count = values.shape[1]
    row_mean = jnp.sum(values, axis=1, keepdims=True) / feature_count
    row_square = jnp.sum(values * values, axis=1, keepdims=True) / feature_count
    scaled = (values - row_mean) * lax.rsqrt(row_square - row_mean * row_mean + EPSILON)
    return (scaled * norm_gain + norm_bias).astype(jnp.bfloat16)


def gathered(hidden, norm_gain, norm_bias, unembed, targets, span_start, span_end):
    slot_count = hidden.shape[0]
    tp_count = lax.axis_size("tp")
    req_rank = lax.axis_index("req")
    tp_rank = lax.axis_index("tp")
    vocab_part = unembed.shape[0]
    vocab_first = (req_rank * tp_count + tp_rank) * vocab_part
    live_mine = live_mask(span_start.reshape(1, -1), span_end.reshape(1, -1), slot_count).reshape(
        -1
    )
    row_ids = lax.all_gather(targets, "req", axis=0, tiled=True)
    full_rows = lax.all_gather(hidden, "tp", axis=1, tiled=True)
    normed = normalize(full_rows, norm_gain, norm_bias)
    scores = lax.dot_general(
        unembed,
        lax.all_gather(normed, "req", axis=0, tiled=True),
        (((1,), (1,)), ((), ())),
        preferred_element_type=jnp.float32,
    )
    vocab_ids = vocab_first + jnp.arange(vocab_part, dtype=jnp.int32)
    target_hit = jnp.sum(jnp.where(vocab_ids[:, None] == row_ids[None, :], scores, 0.0), axis=0)
    row_top = lax.pmax(jnp.max(scores, axis=0), ("req", "tp"))
    weights = jnp.exp(scores - row_top)
    row_total, row_spread, target_hit = lax.psum(
        (jnp.sum(weights, axis=0), jnp.sum(weights * (scores - row_top), axis=0), target_hit),
        ("req", "tp"),
    )
    log_total = jnp.log(row_total)
    logprob_all = target_hit - row_top - log_total
    entropy_all = log_total - row_spread / row_total
    logprob_mine = lax.dynamic_slice_in_dim(logprob_all, req_rank * slot_count, slot_count)
    entropy_mine = lax.dynamic_slice_in_dim(entropy_all, req_rank * slot_count, slot_count)
    return (jnp.where(live_mine, logprob_mine, 0.0), jnp.where(live_mine, entropy_mine, 0.0))


X_BIT, Y_BIT, Z_NEAR, Z_FAR = 1, 2, 4, 8
FAR, FIRST, SECOND = (Z_FAR, Z_FAR), (X_BIT, Y_BIT), (Y_BIT, X_BIT)
LANES = 128
KERNEL_VMEM = 16 << 20
CHUNKS = (24, 40)


def exchange(value, bits):
    pairs = [
        (chip * 2 + core, (chip ^ bits[core]) * 2 + core) for chip in range(16) for core in range(2)
    ]
    return lax.ppermute(value, ("req", "tp"), pairs)


def core_swap(value):
    return lax.ppermute(value, "tp", [(0, 1), (1, 0)])


def in_vmem(value):
    return pltpu.with_memory_space_constraint(value, pltpu.VMEM)


def my_half(ref, half):
    value = ref[...].astype(jnp.float32)
    return jnp.where(lax.axis_index("tp") == 0, value[:half], value[half:])


def stage_kernel(cuts, half, hidden_in, gain_in, bias_in, unembed_in, ids_in, *refs):
    hidden_ref, gain_ref, bias_ref, digit_ref, *chunks = refs[:-2]
    ids_ref, sems = refs[-2:]
    pairs = [(ids_in, ids_ref), (hidden_in, hidden_ref), (gain_in, gain_ref), (bias_in, bias_ref)]
    pairs += [
        (unembed_in.at[pl.ds(start, chunk.shape[0]), :], chunk)
        for chunk, start in zip(chunks, cuts)
    ]
    copies = [pltpu.make_async_copy(*pair, sems.at[k]) for k, pair in enumerate(pairs)]
    for copy in copies:
        copy.start()
    copies[0].wait()
    slots = ids_ref.shape[1]
    slot = lax.axis_index("tp") * half + lax.broadcasted_iota(jnp.int32, (half, slots), 0)
    column = lax.broadcasted_iota(jnp.int32, (half, slots), 1)
    row_ids = jnp.where(slot == column, ids_ref[...], 0).sum(axis=1, keepdims=True)
    lane = lax.broadcasted_iota(jnp.int32, (half, LANES), 1)
    digits = jnp.where(lane == 0, row_ids >> 8, jnp.where(lane == 1, row_ids & 255, 0))
    digit_ref[...] = digits.astype(jnp.float32).astype(jnp.bfloat16)
    for copy in copies[1:]:
        copy.wait()


def in_hbm(value):
    return pltpu.with_memory_space_constraint(value, pltpu.HBM)


def stage(hidden, norm_gain, norm_bias, unembed, targets, cuts):
    half = hidden.shape[0] // 2
    width = norm_gain.shape[0]
    vmem = pl.BlockSpec(memory_space=pltpu.VMEM)
    chunks = [
        pltpu.VMEM((stop - start, width), jnp.bfloat16) for start, stop in zip(cuts, cuts[1:])
    ]
    return pl.pallas_call(
        functools.partial(stage_kernel, cuts, half),
        out_shape=[
            pltpu.VMEM(hidden.shape, hidden.dtype),
            pltpu.VMEM((1, width), jnp.float32),
            pltpu.VMEM((1, width), jnp.float32),
            pltpu.VMEM((half, LANES), jnp.bfloat16),
            *chunks,
        ],
        in_specs=[pl.BlockSpec(memory_space=pltpu.HBM)] * 5,
        out_specs=[vmem] * (4 + len(chunks)),
        scratch_shapes=[
            pltpu.VMEM((1, targets.shape[0]), jnp.int32),
            pltpu.SemaphoreType.DMA((4 + len(chunks),)),
        ],
        compiler_params=pltpu.CompilerParams(vmem_limit_bytes=KERNEL_VMEM),
        name="stage",
    )(
        *map(
            in_hbm,
            (
                hidden,
                norm_gain.reshape(1, -1),
                norm_bias.reshape(1, -1),
                unembed,
                targets.reshape(1, -1),
            ),
        )
    )


def normalize_kernel(own_ref, other_ref, gain_ref, bias_ref, digit_ref, rows_ref):
    half, part = rows_ref.shape[0], own_ref.shape[1]
    first_core = lax.axis_index("tp") == 0
    own, other = my_half(own_ref, half), my_half(other_ref, half)
    low, high = jnp.where(first_core, own, other), jnp.where(first_core, other, own)
    sides = ((low, 0), (high, part))
    row_mean = sum(jnp.sum(side, axis=1, keepdims=True) for side, _ in sides) / (2 * part)
    row_square = sum(jnp.sum(side * side, axis=1, keepdims=True) for side, _ in sides) / (2 * part)
    scale = lax.rsqrt(row_square - row_mean * row_mean + EPSILON)
    for side, start in sides:
        columns = pl.ds(start, part)
        scaled = (side - row_mean) * scale
        rows_ref[:, columns] = (scaled * gain_ref[:, columns] + bias_ref[:, columns]).astype(
            jnp.bfloat16
        )
    rows_ref[:, pl.ds(2 * part, LANES)] = digit_ref[...]


def normalize_rows(own, other, gain, bias, digits):
    half, part = own.shape[0] // 2, own.shape[1]
    vmem = pl.BlockSpec(memory_space=pltpu.VMEM)
    return pl.pallas_call(
        normalize_kernel,
        out_shape=pltpu.VMEM((half, 2 * part + LANES), jnp.bfloat16),
        in_specs=[vmem] * 5,
        out_specs=vmem,
        compiler_params=pltpu.CompilerParams(vmem_limit_bytes=KERNEL_VMEM),
        name="normalize_rows",
    )(*map(in_vmem, (own, other, gain, bias, digits)))


def merge(one, two):
    top = jnp.maximum(one[0], two[0])
    down_one, down_two = one[0] - top, two[0] - top
    scale_one, scale_two = jnp.exp(down_one), jnp.exp(down_two)
    total = scale_one * one[1] + scale_two * two[1]
    spread = scale_one * (one[2] + one[1] * down_one) + scale_two * (two[2] + two[1] * down_two)
    return top, total, spread, one[3] + two[3]


CONTRACT = (((1,), (1,)), ((), ()))


def block_stats(rows_ref, blocks, places, vocab_part):
    width = blocks[0].shape[1]
    row_count = rows_ref.shape[0]
    chip, core = lax.axis_index("req"), lax.axis_index("tp")
    lane = lax.broadcasted_iota(jnp.int32, (16, LANES), 1)
    pick = jnp.where(lane == 0, 256.0, jnp.where(lane == 1, 1.0, 0.0)).astype(jnp.bfloat16)
    row_ids = lax.dot_general(
        pick, rows_ref[:, pl.ds(width, LANES)], CONTRACT, preferred_element_type=jnp.float32
    )[:1].astype(jnp.int32)
    rows = rows_ref[:, pl.ds(0, width)]
    scores = [
        lax.dot_general(block[...], rows, CONTRACT, preferred_element_type=jnp.float32)
        for block in blocks
    ]
    top = scores[0].max(axis=0, keepdims=True)
    for part in scores[1:]:
        top = jnp.maximum(top, part.max(axis=0, keepdims=True))
    total = jnp.zeros((1, row_count), jnp.float32)
    spread, hit = total, total
    for part, (chip_bit, start) in zip(scores, places):
        shifted = part - top
        weights = jnp.exp(shifted)
        total += weights.sum(axis=0, keepdims=True)
        spread += (weights * shifted).sum(axis=0, keepdims=True)
        first = ((chip ^ chip_bit) * 2 + core) * vocab_part + start
        ids = first + lax.broadcasted_iota(jnp.int32, (part.shape[0], 1), 0)
        hit += jnp.where(ids == row_ids, part, 0.0).sum(axis=0, keepdims=True)
    return top, total, spread, hit


def lay(pieces, rows_ref):
    at = 0
    for piece in pieces:
        rows_ref[pl.ds(at, piece.shape[0]), :] = piece[...]
        at += piece.shape[0]


def early_kernel(places, vocab_part, pieces, *refs):
    stats_ref, rows_ref = refs[-2:]
    lay(refs[:pieces], rows_ref)
    stats = block_stats(rows_ref, refs[pieces:-2], places, vocab_part)
    for k in range(4):
        stats_ref[pl.ds(k, 1), :] = stats[k]


def late_kernel(places, vocab_part, early_ref, rows_ref, mine_ref, other_ref, *refs):
    blocks, stats_ref, last_rows_ref = refs[:-2], refs[-2], refs[-1]
    lay((mine_ref, other_ref), last_rows_ref)
    new = block_stats(last_rows_ref, blocks, places, vocab_part)
    rest = block_stats(rows_ref, blocks[-1:], places[-1:], vocab_part)
    old = merge([early_ref[pl.ds(k, 1), :] for k in range(4)], rest)
    old_half, new_half = old[0].shape[1] // 2, new[0].shape[1] // 2
    for k in range(4):
        stats_ref[pl.ds(k, 1), :] = jnp.concatenate(
            [
                old[k][:, :old_half],
                new[k][:, :new_half],
                old[k][:, old_half:],
                new[k][:, new_half:],
            ],
            axis=1,
        )


def early_partials(pieces, blocks, places, vocab_part):
    row_count = len(pieces) * pieces[0].shape[0]
    vmem = pl.BlockSpec(memory_space=pltpu.VMEM)
    return pl.pallas_call(
        functools.partial(early_kernel, places, vocab_part, len(pieces)),
        out_shape=[
            pltpu.VMEM((4, row_count), jnp.float32),
            pltpu.VMEM((row_count, pieces[0].shape[1]), jnp.bfloat16),
        ],
        in_specs=[vmem] * (len(pieces) + len(blocks)),
        out_specs=[vmem] * 2,
        compiler_params=pltpu.CompilerParams(vmem_limit_bytes=KERNEL_VMEM),
        name="early_partials",
    )(*map(in_vmem, (*pieces, *blocks)))


def late_partials(early, rows, mine, other, blocks, places, vocab_part):
    last_count = 2 * mine.shape[0]
    vmem = pl.BlockSpec(memory_space=pltpu.VMEM)
    return pl.pallas_call(
        functools.partial(late_kernel, places, vocab_part),
        out_shape=pltpu.VMEM((4, rows.shape[0] + last_count), jnp.float32),
        in_specs=[vmem] * (4 + len(blocks)),
        out_specs=vmem,
        scratch_shapes=[pltpu.VMEM((last_count, rows.shape[1]), jnp.bfloat16)],
        compiler_params=pltpu.CompilerParams(vmem_limit_bytes=KERNEL_VMEM),
        name="late_partials",
    )(*map(in_vmem, (early, rows, mine, other, *blocks)))


def blocks_of(value, group, order):
    return jnp.concatenate([value[:, at * group : (at + 1) * group] for at in order], axis=1)


def merge_kernel(group, theirs_order, orders, mine_ref, theirs_ref, *outs):
    mine = [mine_ref[pl.ds(k, 1), :] for k in range(4)]
    theirs = [theirs_ref[pl.ds(k, 1), :] for k in range(4)]
    if theirs_order:
        theirs = [blocks_of(value, group, theirs_order) for value in theirs]
    for k, value in enumerate(merge(mine, theirs)):
        for out, order in zip(outs, orders):
            out[pl.ds(k, 1), :] = blocks_of(value, group, order)


def finish_kernel(mine_ref, theirs_ref, out_ref):
    mine, theirs = ([ref[pl.ds(k, 1), :] for k in range(4)] for ref in (mine_ref, theirs_ref))
    row_top, row_total, row_spread, target_hit = merge(mine, theirs)
    log_total = jnp.log(row_total)
    out_ref[pl.ds(0, 1), :] = target_hit - row_top - log_total
    out_ref[pl.ds(1, 1), :] = log_total - row_spread / row_total


def merge_and_split(mine, theirs, group, orders, theirs_order=()):
    vmem = pl.BlockSpec(memory_space=pltpu.VMEM)
    return pl.pallas_call(
        functools.partial(merge_kernel, group, theirs_order, orders),
        out_shape=[pltpu.VMEM((4, group * len(order)), jnp.float32) for order in orders],
        in_specs=[vmem] * 2,
        out_specs=[vmem] * len(orders),
        compiler_params=pltpu.CompilerParams(vmem_limit_bytes=KERNEL_VMEM),
        name="merge_and_split",
    )(in_vmem(mine), in_vmem(theirs))


def finish(mine, theirs):
    vmem = pl.BlockSpec(memory_space=pltpu.VMEM)
    return pl.pallas_call(
        finish_kernel,
        out_shape=pltpu.VMEM((2, mine.shape[1]), jnp.float32),
        in_specs=[vmem] * 2,
        out_specs=vmem,
        compiler_params=pltpu.CompilerParams(vmem_limit_bytes=KERNEL_VMEM),
        name="finish",
    )(in_vmem(mine), in_vmem(theirs))


def paired(hidden, norm_gain, norm_bias, unembed, targets, span_start, span_end):
    slot_count = hidden.shape[0]
    half = slot_count // 2
    vocab_part = unembed.shape[0]
    first_core = lax.axis_index("tp") == 0

    cuts = [0, *[sum(CHUNKS[: k + 1]) for k in range(len(CHUNKS))], vocab_part]
    other = core_swap(hidden)
    own_part, gain, bias, digits, *chunks = stage(
        hidden, norm_gain, norm_bias, unembed, targets, cuts
    )
    own = normalize_rows(own_part, other, gain, bias, digits)
    near = [exchange(chunk, (Z_NEAR, Z_NEAR)) for chunk in chunks]
    far = exchange(own, FAR)
    own_side = exchange(own, FIRST)
    far, own_side, near[0] = lax.optimization_barrier((far, own_side, near[0]))
    near_rows = jnp.concatenate([own, own_side], axis=0)
    near_across = exchange(near_rows, SECOND)
    far_side = exchange(far, FIRST)
    far_side, near_across, near[1] = lax.optimization_barrier((far_side, near_across, near[1]))
    far_rows = jnp.concatenate([far, far_side], axis=0)
    far_across = exchange(far_rows, SECOND)
    far_across, near[2] = lax.optimization_barrier((far_across, near[2]))
    blocks, places = [unembed, *near], [(0, 0)] + [(Z_NEAR, start) for start in cuts[:-1]]
    pieces = [near_rows, far_rows, near_across]
    pieces += [core_swap(piece) for piece in pieces]
    early, rows = early_partials(pieces, blocks[:-1], places[:-1], vocab_part)
    other_across = core_swap(far_across)
    stats = late_partials(early, rows, far_across, other_across, blocks, places, vocab_part)
    swapped = (*range(8, 16), *range(8))
    keep, give = merge_and_split(
        stats,
        core_swap(stats),
        half,
        ((0, 1, 2, 3, 8, 10, 12, 14), (4, 5, 6, 7, 9, 11, 13, 15)),
        swapped,
    )
    keep, give = merge_and_split(
        keep, exchange(give, SECOND), half, ((0, 2, 4, 5), (1, 3, 6, 7))
    )
    keep, give = merge_and_split(keep, exchange(give, FIRST), half, ((0, 2), (1, 3)))
    result = finish(keep, exchange(give, FAR))
    both = jnp.where(
        first_core, result, jnp.concatenate([result[:, half:], result[:, :half]], axis=1)
    )
    live = live_mask(span_start, span_end, slot_count)
    both = jnp.where(live, both, 0.0)
    return both[0], both[1]


def solution(mesh):
    chips_of_two = mesh.shape["req"] == 16 and mesh.shape["tp"] == 2
    return jax.shard_map(
        paired if chips_of_two else gathered,
        mesh=mesh,
        in_specs=(P("req", "tp"), P(), P(), P(("req", "tp"), None), P("req"), P("req"), P("req")),
        out_specs=(P("req"), P("req")),
        check_vma=False,
    )
```

```python
import functools

import jax
import jax.numpy as jnp
from jax import lax
from jax.experimental import pallas as pl
from jax.experimental.pallas import tpu as pltpu
from jax.sharding import PartitionSpec as P

EPSILON = 1e-05


def live_mask(span_start, span_end, slot_count):
    position = jnp.arange(slot_count, dtype=jnp.int32)
    inside = (span_start[..., None] <= position) & (position < span_end[..., None])
    return jnp.any(inside, axis=-2)


def normalize(hidden, norm_gain, norm_bias):
    values = hidden.astype(jnp.float32)
    feature_count = values.shape[1]
    row_mean = jnp.sum(values, axis=1, keepdims=True) / feature_count
    row_square = jnp.sum(values * values, axis=1, keepdims=True) / feature_count
    scaled = (values - row_mean) * lax.rsqrt(row_square - row_mean * row_mean + EPSILON)
    return (scaled * norm_gain + norm_bias).astype(jnp.bfloat16)


def gathered(hidden, norm_gain, norm_bias, unembed, targets, span_start, span_end):
    slot_count = hidden.shape[0]
    tp_count = lax.axis_size("tp")
    req_rank = lax.axis_index("req")
    tp_rank = lax.axis_index("tp")
    vocab_part = unembed.shape[0]
    vocab_first = (req_rank * tp_count + tp_rank) * vocab_part
    live_mine = live_mask(span_start.reshape(1, -1), span_end.reshape(1, -1), slot_count).reshape(
        -1
    )
    row_ids = lax.all_gather(targets, "req", axis=0, tiled=True)
    full_rows = lax.all_gather(hidden, "tp", axis=1, tiled=True)
    normed = normalize(full_rows, norm_gain, norm_bias)
    scores = lax.dot_general(
        unembed,
        lax.all_gather(normed, "req", axis=0, tiled=True),
        (((1,), (1,)), ((), ())),
        preferred_element_type=jnp.float32,
    )
    vocab_ids = vocab_first + jnp.arange(vocab_part, dtype=jnp.int32)
    target_hit = jnp.sum(jnp.where(vocab_ids[:, None] == row_ids[None, :], scores, 0.0), axis=0)
    row_top = lax.pmax(jnp.max(scores, axis=0), ("req", "tp"))
    weights = jnp.exp(scores - row_top)
    row_total, row_spread, target_hit = lax.psum(
        (jnp.sum(weights, axis=0), jnp.sum(weights * (scores - row_top), axis=0), target_hit),
        ("req", "tp"),
    )
    log_total = jnp.log(row_total)
    logprob_all = target_hit - row_top - log_total
    entropy_all = log_total - row_spread / row_total
    logprob_mine = lax.dynamic_slice_in_dim(logprob_all, req_rank * slot_count, slot_count)
    entropy_mine = lax.dynamic_slice_in_dim(entropy_all, req_rank * slot_count, slot_count)
    return (jnp.where(live_mine, logprob_mine, 0.0), jnp.where(live_mine, entropy_mine, 0.0))


X_BIT, Y_BIT, Z_NEAR, Z_FAR = 1, 2, 4, 8
FAR, FIRST, SECOND = (Z_FAR, Z_FAR), (X_BIT, Y_BIT), (Y_BIT, X_BIT)
LANES = 128
KERNEL_VMEM = 16 << 20
CHUNKS = (24, 40)


def exchange(value, bits):
    pairs = [
        (chip * 2 + core, (chip ^ bits[core]) * 2 + core) for chip in range(16) for core in range(2)
    ]
    return lax.ppermute(value, ("req", "tp"), pairs)


def core_swap(value):
    return lax.ppermute(value, "tp", [(0, 1), (1, 0)])


def in_vmem(value):
    return pltpu.with_memory_space_constraint(value, pltpu.VMEM)


def my_half(ref, half):
    value = ref[...].astype(jnp.float32)
    return jnp.where(lax.axis_index("tp") == 0, value[:half], value[half:])


def stage_kernel(cuts, half, hidden_in, gain_in, bias_in, unembed_in, ids_in, *refs):
    hidden_ref, gain_ref, bias_ref, digit_ref, *chunks = refs[:-2]
    ids_ref, sems = refs[-2:]
    pairs = [(ids_in, ids_ref), (hidden_in, hidden_ref), (gain_in, gain_ref), (bias_in, bias_ref)]
    pairs += [
        (unembed_in.at[pl.ds(start, chunk.shape[0]), :], chunk)
        for chunk, start in zip(chunks, cuts)
    ]
    copies = [pltpu.make_async_copy(*pair, sems.at[k]) for k, pair in enumerate(pairs)]
    for copy in copies:
        copy.start()
    copies[0].wait()
    slots = ids_ref.shape[1]
    slot = lax.axis_index("tp") * half + lax.broadcasted_iota(jnp.int32, (half, slots), 0)
    column = lax.broadcasted_iota(jnp.int32, (half, slots), 1)
    row_ids = jnp.where(slot == column, ids_ref[...], 0).sum(axis=1, keepdims=True)
    lane = lax.broadcasted_iota(jnp.int32, (half, LANES), 1)
    digits = jnp.where(lane == 0, row_ids >> 8, jnp.where(lane == 1, row_ids & 255, 0))
    digit_ref[...] = digits.astype(jnp.float32).astype(jnp.bfloat16)
    for copy in copies[1:]:
        copy.wait()


def in_hbm(value):
    return pltpu.with_memory_space_constraint(value, pltpu.HBM)


def stage(hidden, norm_gain, norm_bias, unembed, targets, cuts):
    half = hidden.shape[0] // 2
    width = norm_gain.shape[0]
    vmem = pl.BlockSpec(memory_space=pltpu.VMEM)
    chunks = [
        pltpu.VMEM((stop - start, width), jnp.bfloat16) for start, stop in zip(cuts, cuts[1:])
    ]
    return pl.pallas_call(
        functools.partial(stage_kernel, cuts, half),
        out_shape=[
            pltpu.VMEM(hidden.shape, hidden.dtype),
            pltpu.VMEM((1, width), jnp.float32),
            pltpu.VMEM((1, width), jnp.float32),
            pltpu.VMEM((half, LANES), jnp.bfloat16),
            *chunks,
        ],
        in_specs=[pl.BlockSpec(memory_space=pltpu.HBM)] * 5,
        out_specs=[vmem] * (4 + len(chunks)),
        scratch_shapes=[
            pltpu.VMEM((1, targets.shape[0]), jnp.int32),
            pltpu.SemaphoreType.DMA((4 + len(chunks),)),
        ],
        compiler_params=pltpu.CompilerParams(vmem_limit_bytes=KERNEL_VMEM),
        name="stage",
    )(
        *map(
            in_hbm,
            (
                hidden,
                norm_gain.reshape(1, -1),
                norm_bias.reshape(1, -1),
                unembed,
                targets.reshape(1, -1),
            ),
        )
    )


def normalize_kernel(own_ref, other_ref, gain_ref, bias_ref, digit_ref, rows_ref):
    half, part = rows_ref.shape[0], own_ref.shape[1]
    first_core = lax.axis_index("tp") == 0
    own, other = my_half(own_ref, half), my_half(other_ref, half)
    low, high = jnp.where(first_core, own, other), jnp.where(first_core, other, own)
    sides = ((low, 0), (high, part))
    row_mean = sum(jnp.sum(side, axis=1, keepdims=True) for side, _ in sides) / (2 * part)
    row_square = sum(jnp.sum(side * side, axis=1, keepdims=True) for side, _ in sides) / (2 * part)
    scale = lax.rsqrt(row_square - row_mean * row_mean + EPSILON)
    for side, start in sides:
        columns = pl.ds(start, part)
        scaled = (side - row_mean) * scale
        rows_ref[:, columns] = (scaled * gain_ref[:, columns] + bias_ref[:, columns]).astype(
            jnp.bfloat16
        )
    rows_ref[:, pl.ds(2 * part, LANES)] = digit_ref[...]


def normalize_rows(own, other, gain, bias, digits):
    half, part = own.shape[0] // 2, own.shape[1]
    vmem = pl.BlockSpec(memory_space=pltpu.VMEM)
    return pl.pallas_call(
        normalize_kernel,
        out_shape=pltpu.VMEM((half, 2 * part + LANES), jnp.bfloat16),
        in_specs=[vmem] * 5,
        out_specs=vmem,
        compiler_params=pltpu.CompilerParams(vmem_limit_bytes=KERNEL_VMEM),
        name="normalize_rows",
    )(*map(in_vmem, (own, other, gain, bias, digits)))


def merge(one, two):
    top = jnp.maximum(one[0], two[0])
    down_one, down_two = one[0] - top, two[0] - top
    scale_one, scale_two = jnp.exp(down_one), jnp.exp(down_two)
    total = scale_one * one[1] + scale_two * two[1]
    spread = scale_one * (one[2] + one[1] * down_one) + scale_two * (two[2] + two[1] * down_two)
    return top, total, spread, one[3] + two[3]


CONTRACT = (((1,), (1,)), ((), ()))


def block_stats(rows_ref, blocks, places, vocab_part):
    width = blocks[0].shape[1]
    row_count = rows_ref.shape[0]
    chip, core = lax.axis_index("req"), lax.axis_index("tp")
    lane = lax.broadcasted_iota(jnp.int32, (16, LANES), 1)
    pick = jnp.where(lane == 0, 256.0, jnp.where(lane == 1, 1.0, 0.0)).astype(jnp.bfloat16)
    row_ids = lax.dot_general(
        pick, rows_ref[:, pl.ds(width, LANES)], CONTRACT, preferred_element_type=jnp.float32
    )[:1].astype(jnp.int32)
    rows = rows_ref[:, pl.ds(0, width)]
    scores = [
        lax.dot_general(block[...], rows, CONTRACT, preferred_element_type=jnp.float32)
        for block in blocks
    ]
    top = scores[0].max(axis=0, keepdims=True)
    for part in scores[1:]:
        top = jnp.maximum(top, part.max(axis=0, keepdims=True))
    total = jnp.zeros((1, row_count), jnp.float32)
    spread, hit = total, total
    for part, (chip_bit, start) in zip(scores, places):
        shifted = part - top
        weights = jnp.exp(shifted)
        total += weights.sum(axis=0, keepdims=True)
        spread += (weights * shifted).sum(axis=0, keepdims=True)
        first = ((chip ^ chip_bit) * 2 + core) * vocab_part + start
        ids = first + lax.broadcasted_iota(jnp.int32, (part.shape[0], 1), 0)
        hit += jnp.where(ids == row_ids, part, 0.0).sum(axis=0, keepdims=True)
    return top, total, spread, hit


def lay(pieces, rows_ref):
    at = 0
    for piece in pieces:
        rows_ref[pl.ds(at, piece.shape[0]), :] = piece[...]
        at += piece.shape[0]


def early_kernel(places, vocab_part, pieces, *refs):
    stats_ref, rows_ref = refs[-2:]
    lay(refs[:pieces], rows_ref)
    stats = block_stats(rows_ref, refs[pieces:-2], places, vocab_part)
    for k in range(4):
        stats_ref[pl.ds(k, 1), :] = stats[k]


def late_kernel(places, vocab_part, early_ref, rows_ref, mine_ref, other_ref, *refs):
    blocks, stats_ref, last_rows_ref = refs[:-2], refs[-2], refs[-1]
    lay((mine_ref, other_ref), last_rows_ref)
    new = block_stats(last_rows_ref, blocks, places, vocab_part)
    rest = block_stats(rows_ref, blocks[-1:], places[-1:], vocab_part)
    old = merge([early_ref[pl.ds(k, 1), :] for k in range(4)], rest)
    old_half, new_half = old[0].shape[1] // 2, new[0].shape[1] // 2
    for k in range(4):
        stats_ref[pl.ds(k, 1), :] = jnp.concatenate(
            [
                old[k][:, :old_half],
                new[k][:, :new_half],
                old[k][:, old_half:],
                new[k][:, new_half:],
            ],
            axis=1,
        )


def early_partials(pieces, blocks, places, vocab_part):
    row_count = len(pieces) * pieces[0].shape[0]
    vmem = pl.BlockSpec(memory_space=pltpu.VMEM)
    return pl.pallas_call(
        functools.partial(early_kernel, places, vocab_part, len(pieces)),
        out_shape=[
            pltpu.VMEM((4, row_count), jnp.float32),
            pltpu.VMEM((row_count, pieces[0].shape[1]), jnp.bfloat16),
        ],
        in_specs=[vmem] * (len(pieces) + len(blocks)),
        out_specs=[vmem] * 2,
        compiler_params=pltpu.CompilerParams(vmem_limit_bytes=KERNEL_VMEM),
        name="early_partials",
    )(*map(in_vmem, (*pieces, *blocks)))


def late_partials(early, rows, mine, other, blocks, places, vocab_part):
    last_count = 2 * mine.shape[0]
    vmem = pl.BlockSpec(memory_space=pltpu.VMEM)
    return pl.pallas_call(
        functools.partial(late_kernel, places, vocab_part),
        out_shape=pltpu.VMEM((4, rows.shape[0] + last_count), jnp.float32),
        in_specs=[vmem] * (4 + len(blocks)),
        out_specs=vmem,
        scratch_shapes=[pltpu.VMEM((last_count, rows.shape[1]), jnp.bfloat16)],
        compiler_params=pltpu.CompilerParams(vmem_limit_bytes=KERNEL_VMEM),
        name="late_partials",
    )(*map(in_vmem, (early, rows, mine, other, *blocks)))


def blocks_of(value, group, order):
    return jnp.concatenate([value[:, at * group : (at + 1) * group] for at in order], axis=1)


def merge_kernel(group, theirs_order, orders, mine_ref, theirs_ref, *outs):
    mine = [mine_ref[pl.ds(k, 1), :] for k in range(4)]
    theirs = [theirs_ref[pl.ds(k, 1), :] for k in range(4)]
    if theirs_order:
        theirs = [blocks_of(value, group, theirs_order) for value in theirs]
    for k, value in enumerate(merge(mine, theirs)):
        for out, order in zip(outs, orders):
            out[pl.ds(k, 1), :] = blocks_of(value, group, order)


def finish_kernel(mine_ref, theirs_ref, live_ref, logprob_ref, entropy_ref):
    mine, theirs = ([ref[pl.ds(k, 1), :] for k in range(4)] for ref in (mine_ref, theirs_ref))
    row_top, row_total, row_spread, target_hit = merge(mine, theirs)
    log_total = jnp.log(row_total)
    half = mine_ref.shape[1] // 2
    results = (target_hit - row_top - log_total, log_total - row_spread / row_total)
    for value, out in zip(results, (logprob_ref, entropy_ref)):
        turned = blocks_of(value, half, (1, 0))
        value = jnp.where(lax.axis_index("tp") == 0, value, turned)
        out[...] = jnp.where(live_ref[...] > 0, value, 0.0)


def merge_and_split(mine, theirs, group, orders, theirs_order=()):
    vmem = pl.BlockSpec(memory_space=pltpu.VMEM)
    return pl.pallas_call(
        functools.partial(merge_kernel, group, theirs_order, orders),
        out_shape=[pltpu.VMEM((4, group * len(order)), jnp.float32) for order in orders],
        in_specs=[vmem] * 2,
        out_specs=[vmem] * len(orders),
        compiler_params=pltpu.CompilerParams(vmem_limit_bytes=KERNEL_VMEM),
        name="merge_and_split",
    )(in_vmem(mine), in_vmem(theirs))


def finish(mine, theirs, live):
    vmem = pl.BlockSpec(memory_space=pltpu.VMEM)
    return pl.pallas_call(
        finish_kernel,
        out_shape=[jax.ShapeDtypeStruct((1, mine.shape[1]), jnp.float32)] * 2,
        in_specs=[vmem] * 3,
        out_specs=[vmem] * 2,
        compiler_params=pltpu.CompilerParams(vmem_limit_bytes=KERNEL_VMEM),
        name="finish",
    )(in_vmem(mine), in_vmem(theirs), in_vmem(live))


def paired(hidden, norm_gain, norm_bias, unembed, targets, span_start, span_end):
    slot_count = hidden.shape[0]
    half = slot_count // 2
    vocab_part = unembed.shape[0]

    cuts = [0, *[sum(CHUNKS[: k + 1]) for k in range(len(CHUNKS))], vocab_part]
    other = core_swap(hidden)
    own_part, gain, bias, digits, *chunks = stage(
        hidden, norm_gain, norm_bias, unembed, targets, cuts
    )
    own = normalize_rows(own_part, other, gain, bias, digits)
    near = [exchange(chunk, (Z_NEAR, Z_NEAR)) for chunk in chunks]
    far = exchange(own, FAR)
    own_side = exchange(own, FIRST)
    far, own_side, near[0] = lax.optimization_barrier((far, own_side, near[0]))
    near_rows = jnp.concatenate([own, own_side], axis=0)
    near_across = exchange(near_rows, SECOND)
    far_side = exchange(far, FIRST)
    far_side, near_across, near[1] = lax.optimization_barrier((far_side, near_across, near[1]))
    far_rows = jnp.concatenate([far, far_side], axis=0)
    far_across = exchange(far_rows, SECOND)
    far_across, near[2] = lax.optimization_barrier((far_across, near[2]))
    blocks, places = [unembed, *near], [(0, 0)] + [(Z_NEAR, start) for start in cuts[:-1]]
    pieces = [near_rows, far_rows, near_across]
    pieces += [core_swap(piece) for piece in pieces]
    early, rows = early_partials(pieces, blocks[:-1], places[:-1], vocab_part)
    other_across = core_swap(far_across)
    stats = late_partials(early, rows, far_across, other_across, blocks, places, vocab_part)
    swapped = (*range(8, 16), *range(8))
    keep, give = merge_and_split(
        stats,
        core_swap(stats),
        half,
        ((0, 1, 2, 3, 8, 10, 12, 14), (4, 5, 6, 7, 9, 11, 13, 15)),
        swapped,
    )
    keep, give = merge_and_split(
        keep, exchange(give, SECOND), half, ((0, 2, 4, 5), (1, 3, 6, 7))
    )
    keep, give = merge_and_split(keep, exchange(give, FIRST), half, ((0, 2), (1, 3)))
    live = live_mask(span_start, span_end, slot_count).astype(jnp.int32).reshape(1, -1)
    logprob, entropy = finish(keep, exchange(give, FAR), live)
    return logprob.reshape(-1), entropy.reshape(-1)


def solution(mesh):
    chips_of_two = mesh.shape["req"] == 16 and mesh.shape["tp"] == 2
    return jax.shard_map(
        paired if chips_of_two else gathered,
        mesh=mesh,
        in_specs=(P("req", "tp"), P(), P(), P(("req", "tp"), None), P("req"), P("req"), P("req")),
        out_specs=(P("req"), P("req")),
        check_vma=False,
    )
```
